256 devices in a mesh: sec: 4 (over y), comp: 64 (over x, z, core).
Axes of the slice: x: 4, y: 4, z: 8, core: 2. Of those that a mesh axis runs over, the one named last changes fastest.
Arguments:
- spectrum: float32 [96, 384, 1152], P('sec', 'comp'), may hold values from 0.05 to 2
- land: int32 [96, 384], P('sec', 'comp'), may hold values 0 or 1
- currents: float32 [2, 96, 384], P(None, 'sec', 'comp'), may hold values from -0.2 to 0.2
- group_courant: float32 [32], replicated, may hold values from 0.05 to 0.4
- w_gate: bfloat16 [1152, 1152], replicated, may hold values from -0.1875 to 0.1875
- w_up: bfloat16 [1152, 1152], replicated, may hold values from -0.1875 to 0.1875
- w_down: bfloat16 [1152, 1152], replicated, may hold values from -0.1875 to 0.1875
- stokes_profile: bfloat16 [1152, 80], replicated, may hold values from -0.1875 to 0.1875
- ocean_vel: float32 [2, 40, 96, 384], P(None, None, 'sec', 'comp'), may hold values from -3 to 3
- mixing: float32 [40], replicated, may hold values from 0.05 to 0.3
Outputs:
- spectrum_next: float32 [96, 384, 1152], P('sec', 'comp')
- ocean_next: float32 [2, 40, 96, 384], P(None, None, 'sec', 'comp')
The draws below stay inside these ranges and needn't reach their ends.
Inputs may be any that keep to these rules, and one draw needn't show every extreme that they name: 1 marks a sea point, 0 a land point.
All inputs are finite; a program needn't handle non-finite values. No bound on the sum of `land` on one device may be relied on, other than what follows from the above.
Results may differ from the reference program's by a relative error of at most 0.002.
Values sent between devices are 32-bit elements; how exact they have to be, the bound alone decides.
No kernel may reach another device: no remote copies, remote signals or barrier semaphores. Data moves between devices by JAX's collectives and lax.ppermute only.
A program may use at most 128 MiB of HBM per device.

```python
import math
import jax
import jax.numpy as jnp
from jax import lax

DIRS = 36
FREQS = 32
K = 1152
LAYERS = 40
SUBSTEPS = 4
STEPS = 3
NLAT = 96
NLON = 384


def touch_ends(values, rng, low, largest):
    longest = values.shape.index(max(values.shape))
    spots = []
    for shift in (0, 1):
        where = [jax.random.randint(jax.random.fold_in(rng, axis), (), 0, length) for axis, length in enumerate(values.shape)]
        where[longest] = (where[longest] + shift) % values.shape[longest]
        spots.append(tuple(where))
    return values.at[spots[0]].set(low).at[spots[1]].set(largest)


def level_of(rng, shape, split, least, largest):
    def one(position, parts):
        steps = jax.random.uniform(jax.random.fold_in(jax.random.fold_in(rng, 6), position), (parts,), jnp.float32, least / len(split), largest / len(split))
        return jnp.repeat(jnp.exp(steps), shape[position] // parts).reshape((-1,) + (1,) * (len(shape) - position - 1))

    loudness = one(*split[0])
    for cut in split[1:]:
        loudness = loudness * one(*cut)
    return loudness


def scatter_about(rng, shape, width, most, shards=(), held_as=jnp.bfloat16):
    result = width * jax.random.normal(rng, shape, jnp.float32)
    if shards:
        result = result * level_of(rng, shape, shards, -0.22, 0.18)
    return jnp.clip(result, -most, most).astype(held_as)


def setup_inputs(seed: int = 0) -> dict:
    key_list = jax.random.split(jax.random.key(seed), 11)
    spectrum = jnp.clip(jnp.exp(math.log(2.0) - 3.6888794 * jax.random.uniform(key_list[0], (NLAT, NLON, K), jnp.float32) ** level_of(key_list[0], (NLAT, NLON, K), ((0, 4), (1, 64)), -0.2, 0.2)), 0.05, 2.0)
    land = touch_ends((jax.random.randint(key_list[1], (NLAT, NLON), 0, 4) < 3).astype(jnp.int32), jax.random.fold_in(key_list[1], 1), 0, 1)
    currents = jnp.clip(jax.random.uniform(key_list[2], (2, NLAT, NLON), jnp.float32, -0.2, 0.2) * level_of(key_list[2], (2, NLAT, NLON), ((1, 4), (2, 64)), -0.4, 0.0), -0.2, 0.2)
    group_courant = jnp.clip(jnp.exp(jax.random.uniform(key_list[3], (FREQS,), jnp.float32, math.log(0.05), math.log(0.4))), 0.05, 0.4)
    w_gate = scatter_about(key_list[4], (K, K), K ** -0.5, 0.1875)
    w_up = scatter_about(key_list[5], (K, K), K ** -0.5, 0.1875)
    w_down = scatter_about(key_list[6], (K, K), K ** -0.5, 0.1875)
    stokes_profile = scatter_about(key_list[7], (K, 2 * LAYERS), K ** -0.5, 0.1875)
    ocean_vel = scatter_about(key_list[8], (2, LAYERS, NLAT, NLON), 0.5, 3.0, ((2, 4), (3, 64)), jnp.float32)
    mixing = jnp.clip(jnp.exp(jax.random.uniform(key_list[9], (LAYERS,), jnp.float32, math.log(0.05), math.log(0.3))), 0.05, 0.3)
    return {"spectrum": spectrum, "land": land, "currents": currents, "group_courant": group_courant, "w_gate": w_gate, "w_up": w_up, "w_down": w_down, "stokes_profile": stokes_profile, "ocean_vel": ocean_vel, "mixing": mixing}


def upwind(core, west, east, south, north, cx, cy, wet):
    return wet * (core - jnp.maximum(cx, 0.0) * (core - west) - jnp.minimum(cx, 0.0) * (east - core)
                  - jnp.maximum(cy, 0.0) * (core - south) - jnp.minimum(cy, 0.0) * (north - core))


def ocean_update(vel, stokes, wet, coriolis, mixing):
    lower = jnp.concatenate([vel[:, :1], vel[:, :-1]], axis=1)
    upper = jnp.concatenate([vel[:, 1:], vel[:, -1:]], axis=1)
    lap = lower - 2.0 * vel + upper
    kappa = mixing[:, None, None]
    rate = 0.5 * coriolis[:, None]
    east = wet * (vel[0] + kappa * lap[0] + rate * (vel[1] + stokes[1]))
    north = wet * (vel[1] + kappa * lap[1] - rate * (vel[0] + stokes[0]))
    return jnp.stack([east, north], axis=0)


def reference(spectrum, land, currents, group_courant, w_gate, w_up, w_down, stokes_profile, ocean_vel, mixing):
    wet = land.astype(jnp.float32)
    theta = 2.0 * math.pi * (jnp.arange(DIRS).astype(jnp.float32) + 0.5) / DIRS
    rows = jnp.arange(NLAT).astype(jnp.float32)
    coriolis = jnp.sin((rows + 0.5) * (math.pi / NLAT) - math.pi / 2)
    spec = spectrum
    ocean = ocean_vel
    surf = currents
    for outer in range(STEPS):
        start = spec * wet[:, :, None]
        by_freq = start.reshape(NLAT, NLON, FREQS, DIRS).transpose(2, 0, 1, 3)

        def advect(item):
            field, speed = item
            cx = (speed * jnp.cos(theta))[None, None, :] + surf[0][:, :, None]
            cy = (speed * jnp.sin(theta))[None, None, :] + surf[1][:, :, None]
            for step in range(SUBSTEPS):
                padded = jnp.pad(field, ((1, 1), (0, 0), (0, 0)))
                field = upwind(field, jnp.roll(field, 1, axis=1), jnp.roll(field, -1, axis=1),
                               padded[:-2], padded[2:], cx, cy, wet[:, :, None])
            return field

        advected = lax.map(advect, (by_freq, group_courant))
        advected = advected.transpose(1, 2, 0, 3).reshape(NLAT, NLON, K)

        def sources(item):
            row, wet_row = item
            rounded = row.astype(jnp.bfloat16)
            gate = jnp.dot(rounded, w_gate, preferred_element_type=jnp.float32)
            up = jnp.dot(rounded, w_up, preferred_element_type=jnp.float32)
            hidden = (jax.nn.silu(gate) * up).astype(jnp.bfloat16)
            source = jnp.dot(hidden, w_down, preferred_element_type=jnp.float32)
            fresh = wet_row[:, None] * (row + source)
            drift = jnp.dot(fresh.astype(jnp.bfloat16), stokes_profile, preferred_element_type=jnp.float32)
            return fresh, drift

        spec, drift = lax.map(sources, (advected, wet))
        stokes = drift.transpose(2, 0, 1).reshape(2, LAYERS, NLAT, NLON)
        ocean = ocean_update(ocean, stokes, wet, coriolis, mixing)
        surf = 0.2 * jnp.tanh(ocean[:, 0])
    return spec, ocean
```

```python
import functools
import math

import jax
import jax.numpy as jnp
from jax import lax
from jax.experimental import pallas as pl
from jax.experimental.pallas import tpu as pltpu
from jax.sharding import PartitionSpec as P

DIRS = 36
FREQS = 32
K = DIRS * FREQS
LAYERS = 40
SUBSTEPS = 4
STEPS = 3
HALO = SUBSTEPS
LANES = 128
WET = 80
RATE = 81
CHUNK = 384


def shrink(x, rows):
    if rows == 48:
        return jnp.concatenate([x[:32], x[40:]], axis=0)
    if rows == 40:
        low = lax.broadcasted_iota(jnp.int32, (8, x.shape[1]), 0) < 4
        return jnp.concatenate([x[:24], jnp.where(low, x[24:32], x[32:])], axis=0)
    return x[:24]


def wide(x, lane):
    return jnp.broadcast_to(x[:, lane : lane + 1], (x.shape[0], LANES))


def pack_aux(cols, rows):
    tiles = rows // 8
    lane = lax.broadcasted_iota(jnp.int32, (8, LANES), 1)
    out = jnp.zeros((8, LANES), jnp.float32)
    for c, col in enumerate(cols):
        for t in range(tiles):
            part = col[8 * t : 8 * t + 8]
            first = 3 * (c * tiles + t)
            for k, source in enumerate((0, LAYERS, WET)):
                out = jnp.where(lane == first + k, wide(part, source), out)
    return out


def fill_messages(spec, aux, e_out, w_out, rows):
    for out, first in ((e_out, 2), (w_out, 0)):
        for c in range(HALO):
            out[c * rows : (c + 1) * rows, :] = spec[first + c]
        out[HALO * rows :, :LANES] = pack_aux([aux[first + c] for c in range(HALO)], rows)


def pack_kernel(rows, spec, aux, e_out, w_out):
    fill_messages(spec, aux, e_out, w_out, rows)


def step_kernel(rows, last, *refs):
    (spec, aux, ocean, from_w, from_e, speeds, mixing, w_gate, w_up, w_down, profile) = refs[:11]
    if last:
        spec_out, ocean_out = refs[11:13]
        rest = refs[13:]
    else:
        spec_out, aux_out, ocean_out, e_out, w_out = refs[11:16]
        rest = refs[16:]
    s0, s1, wet, coef, field, act, hidden = rest
    tiles = rows // 8
    fewer = rows - 2 * HALO
    columns = 6 + 2 * HALO

    for c in range(columns):
        if HALO <= c < columns - HALO:
            x = aux[c - HALO]
            s0[c] = wide(x, 0)
            s1[c] = wide(x, LAYERS)
            wet[c] = wide(x, WET)
        else:
            message, k = (from_w, c) if c < HALO else (from_e, c - HALO - 6)
            x = message[HALO * rows :, :LANES]
            for t in range(tiles):
                first = 3 * (k * tiles + t)
                at = pl.ds(8 * t, 8)
                s0[c, at] = wide(x, first)
                s1[c, at] = wide(x, first + 1)
                wet[c, at] = wide(x, first + 2)

    def advect(j, _):
        at = pl.ds(pl.multiple_of(j * LANES, LANES), LANES)
        along_x = speeds[0:1, at]
        along_y = speeds[1:2, at]

        def start(c):
            if c < HALO:
                return from_w[c * rows : (c + 1) * rows, at]
            if c < HALO + 6:
                return spec[c - HALO, :, at]
            return from_e[(c - HALO - 6) * rows : (c - HALO - 5) * rows, at]

        for c in range(1, columns - 1):
            w = wet[c]
            cx = along_x + s0[c]
            cy = along_y + s1[c]
            west = w * jnp.maximum(cx, 0.0)
            east = w * jnp.maximum(-cx, 0.0)
            south = w * jnp.maximum(cy, 0.0)
            north = w * jnp.maximum(-cy, 0.0)
            coef[0, c] = w - ((west + east) + (south + north))
            coef[1, c] = west
            coef[2, c] = east
            coef[3, c] = south
            coef[4, c] = north
        for sub in range(SUBSTEPS):
            read = start if sub == 0 else (lambda c, b=(sub - 1) % 2: field[b, c])
            before = read(sub)
            here = read(sub + 1)
            for c in range(sub + 1, columns - sub - 1):
                after = read(c + 1)
                new = (
                    coef[0, c] * here
                    + coef[1, c] * before
                    + coef[2, c] * after
                    + coef[3, c] * pltpu.roll(here, 1, 0)
                    + coef[4, c] * pltpu.roll(here, rows - 1, 0)
                )
                if sub < SUBSTEPS - 1:
                    field[sub % 2, c] = new
                else:
                    spec_out[c - HALO, :, at] = shrink(new, rows)
                before, here = here, after
        return 0

    lax.fori_loop(0, K // LANES, advect, 0)

    for c in range(6):
        act[c * fewer : (c + 1) * fewer, :] = spec_out[c].astype(jnp.bfloat16)
    for n in range(0, K, CHUNK):
        a = act[...]
        gate = jnp.dot(a, w_gate[:, n : n + CHUNK], preferred_element_type=jnp.float32)
        up = jnp.dot(a, w_up[:, n : n + CHUNK], preferred_element_type=jnp.float32)
        hidden[:, n : n + CHUNK] = (jax.nn.silu(gate) * up).astype(jnp.bfloat16)
    for n in range(0, K, CHUNK):
        source = jnp.dot(hidden[...], w_down[:, n : n + CHUNK], preferred_element_type=jnp.float32)
        for c in range(6):
            mask = shrink(wet[c + HALO], rows)[:, :1]
            at = pl.ds(c * fewer, fewer)
            fresh = mask * (spec_out[c, :, n : n + CHUNK] + source[c * fewer : (c + 1) * fewer])
            spec_out[c, :, n : n + CHUNK] = fresh
            act[at, n : n + CHUNK] = fresh.astype(jnp.bfloat16)
    stokes = jnp.dot(act[...], profile[...], preferred_element_type=jnp.float32)

    lane = lax.broadcasted_iota(jnp.int32, (fewer, LANES), 1)
    first = lane < LAYERS
    kappa = mixing[...]
    for c in range(6):
        v = shrink(ocean[c], rows)
        known = shrink(aux[c], rows)
        lower = jnp.where((lane == 0) | (lane == LAYERS), v, pltpu.roll(v, 1, 1))
        upper = jnp.where((lane == LAYERS - 1) | (lane == 2 * LAYERS - 1), v, pltpu.roll(v, LANES - 1, 1))
        lap = lower - 2.0 * v + upper
        moved = v + stokes[c * fewer : (c + 1) * fewer]
        other = jnp.where(first, pltpu.roll(moved, LANES - LAYERS, 1), -pltpu.roll(moved, LAYERS, 1))
        new = wide(known, WET) * (v + kappa * lap + wide(known, RATE) * other)
        ocean_out[c] = new
        if not last:
            aux_out[c] = jnp.where(lane < 2 * LAYERS, 0.2 * jnp.tanh(new), known)
    if not last:
        fill_messages(spec_out, aux_out, e_out, w_out, fewer)


def kernel_call(body, outs, scratch, *args, flops=0):
    block = pl.BlockSpec(memory_space=pltpu.VMEM)
    return pl.pallas_call(
        body,
        out_shape=[jax.ShapeDtypeStruct(shape, jnp.float32) for shape in outs],
        in_specs=[block] * len(args),
        out_specs=[block] * len(outs),
        scratch_shapes=scratch,
        compiler_params=pltpu.CompilerParams(vmem_limit_bytes=30 << 20),
        cost_estimate=pl.CostEstimate(flops=flops, bytes_accessed=10 << 20, transcendentals=0),
    )(*args)


def shards(
    spectrum, land, currents, group_courant, w_gate, w_up, w_down, stokes_profile, ocean_vel, mixing
):
    rows, columns, _ = spectrum.shape
    far = STEPS * HALO
    bands, sectors = lax.axis_size("sec"), lax.axis_size("comp")
    band = lax.axis_index("sec")
    up = [(i, (i + 1) % bands) for i in range(bands)]
    down = [(b, a) for a, b in up]
    east = [(i, (i + 1) % sectors) for i in range(sectors)]
    west = [(b, a) for a, b in east]

    theta = 2.0 * math.pi * (jnp.arange(DIRS).astype(jnp.float32) + 0.5) / DIRS
    speed = jnp.repeat(group_courant, DIRS)
    speeds = jnp.stack([speed * jnp.tile(jnp.cos(theta), FREQS), speed * jnp.tile(jnp.sin(theta), FREQS)])
    speeds = jnp.pad(speeds, ((0, 6), (0, 0)))
    kappa = jnp.pad(jnp.concatenate([mixing, mixing]), (0, LANES - 2 * LAYERS))[None, :]
    profile = jnp.pad(stokes_profile, ((0, 0), (0, LANES - 2 * LAYERS)))

    wet = land.astype(jnp.float32)
    spec = (spectrum * wet[:, :, None]).transpose(1, 0, 2)
    ocean = ocean_vel.transpose(3, 2, 0, 1).reshape(columns, rows, 2 * LAYERS)
    more = jnp.concatenate([wet.T[:, :, None], jnp.moveaxis(currents, 0, 2).transpose(1, 0, 2)], axis=2)
    more = jnp.concatenate([ocean, more, jnp.zeros((columns, rows, LANES - 2 * LAYERS - 3), jnp.float32)], axis=2)
    both = jnp.concatenate([spec, more], axis=2)
    low = lax.ppermute(both[:, rows - far :].reshape(columns * far, -1), "sec", up)
    high = lax.ppermute(both[:, :far].reshape(columns * far, -1), "sec", down)
    low = jnp.where(band == 0, 0.0, low).reshape(columns, far, -1)
    high = jnp.where(band == bands - 1, 0.0, high).reshape(columns, far, -1)
    both = jnp.concatenate([both, high, low], axis=1)
    spec, more = both[:, :, :K], both[:, :, K:]
    tall = rows + 2 * far
    places = jnp.concatenate([jnp.arange(rows + far), jnp.arange(-far, 0)])
    places = (band * rows + places).astype(jnp.float32)
    rate = 0.5 * jnp.sin((places + 0.5) * (math.pi / (rows * bands)) - math.pi / 2)
    lane = jnp.arange(LANES)
    ocean = jnp.where(lane < 2 * LAYERS, more, 0.0)
    aux = jnp.where(
        lane == 0, more[:, :, 81:82], jnp.where(lane == LAYERS, more[:, :, 82:83], more[:, :, 80:81])
    )
    aux = jnp.where(lane == RATE, rate[None, :, None], aux)

    message = (HALO * tall + 8, K)
    e_out, w_out = kernel_call(functools.partial(pack_kernel, tall), [message] * 2, [], spec, aux)
    for step in range(STEPS):
        last = step == STEPS - 1
        from_w = lax.ppermute(e_out, "comp", east)
        from_e = lax.ppermute(w_out, "comp", west)
        fewer = tall - 2 * HALO
        ext = columns + 2 * HALO
        scratch = [pltpu.VMEM((ext, tall, LANES), jnp.float32)] * 3 + [
            pltpu.VMEM((5, ext, tall, LANES), jnp.float32),
            pltpu.VMEM((2, ext, tall, LANES), jnp.float32),
            pltpu.VMEM((columns * fewer, K), jnp.bfloat16),
            pltpu.VMEM((columns * fewer, K), jnp.bfloat16),
        ]
        small = (columns, fewer, LANES)
        message = (HALO * fewer + 8, K)
        outs = [(columns, fewer, K), small] if last else [(columns, fewer, K), small, small, message, message]
        result = kernel_call(
            functools.partial(step_kernel, tall, last),
            outs,
            scratch,
            spec, aux, ocean, from_w, from_e, speeds, kappa, w_gate, w_up, w_down, profile,
            flops=6 * columns * fewer * K * K,
        )
        if last:
            spec, ocean = result
        else:
            spec, aux, ocean, e_out, w_out = result
        tall = fewer
    spec = spec.transpose(1, 0, 2)
    ocean = ocean[:, :, : 2 * LAYERS].reshape(columns, rows, 2, LAYERS).transpose(2, 3, 1, 0)
    return spec, ocean


def solution(mesh):
    return jax.shard_map(
        shards,
        mesh=mesh,
        in_specs=(
            P("sec", "comp", None),
            P("sec", "comp"),
            P(None, "sec", "comp"),
            P(),
            P(),
            P(),
            P(),
            P(),
            P(None, None, "sec", "comp"),
            P(),
        ),
        out_specs=(P("sec", "comp", None), P(None, None, "sec", "comp")),
        check_vma=False,
    )
```

```python
import functools
import math

import jax
import jax.numpy as jnp
from jax import lax
from jax.experimental import pallas as pl
from jax.experimental.pallas import tpu as pltpu
from jax.sharding import PartitionSpec as P

DIRS = 36
FREQS = 32
K = DIRS * FREQS
LAYERS = 40
SUBSTEPS = 4
STEPS = 3
HALO = SUBSTEPS
FAR = STEPS * HALO
OWN = 6
EXT = OWN + 2 * HALO
LANES = 128
WET = 80
RATE = 81
CHUNK = 384
HALVES = ((0, 640), (640, 512))


def shrink(x, rows):
    if rows == 48:
        return jnp.concatenate([x[:32], x[40:]], axis=0)
    if rows == 40:
        low = lax.broadcasted_iota(jnp.int32, (8, x.shape[1]), 0) < 4
        return jnp.concatenate([x[:24], jnp.where(low, x[24:32], x[32:])], axis=0)
    return x[:24]


def wide(x, lane):
    return jnp.broadcast_to(x[:, lane : lane + 1], (x.shape[0], LANES))


def pack_aux(cols, rows):
    tiles = rows // 8
    lane = lax.broadcasted_iota(jnp.int32, (8, LANES), 1)
    out = jnp.zeros((8, LANES), jnp.float32)
    for c, col in enumerate(cols):
        for t in range(tiles):
            part = col[8 * t : 8 * t + 8]
            first = 3 * (c * tiles + t)
            for k, source in enumerate((0, LAYERS, WET)):
                out = jnp.where(lane == first + k, wide(part, source), out)
    return out


def fill_messages(spec, aux, outs, rows):
    for side, first in ((0, 2), (1, 0)):
        for half, (start, width) in enumerate(HALVES):
            out = outs[2 * side + half]
            for c in range(HALO):
                out[c * rows : (c + 1) * rows, :] = spec[first + c, :, start : start + width]
        if aux is not None:
            columns = [aux[first + c] for c in range(HALO)]
            outs[2 * side][HALO * rows :, :LANES] = pack_aux(columns, columns[0].shape[0])


def message_shapes(rows, extra=8):
    sizes = [(HALO * rows + (0 if half else extra), width) for half, (_, width) in enumerate(HALVES)]
    return sizes * 2


def pack_rows(spec, low, high):
    rows = spec.shape[1]
    for c in range(OWN):
        at = pl.ds(c * FAR, FAR)
        low[at] = spec[c, rows - FAR :]
        high[at] = spec[c, :FAR]


def pack_own(spec, *outs):
    fill_messages(spec, None, outs, spec.shape[1])


def pack_far(low, high, more_low, more_high, keep, rate, more, spec_out, aux_out, ocean_out, *outs):
    rows = more.shape[1]
    lane = lax.broadcasted_iota(jnp.int32, (rows + 2 * FAR, LANES), 1)
    keep_low, keep_high = keep[0:1, :1], keep[1:2, :1]
    for c in range(OWN):
        at = pl.ds(c * FAR, FAR)
        spec_out[c, :FAR] = high[at] * keep_high
        spec_out[c, FAR:] = low[at] * keep_low
        ocean_out[c, :rows] = more[c]
        ocean_out[c, rows : rows + FAR] = more_high[at] * keep_high
        ocean_out[c, rows + FAR :] = more_low[at] * keep_low
        x = ocean_out[c]
        x = jnp.where(lane == 0, wide(x, 82), jnp.where(lane == LAYERS, wide(x, 83), x))
        aux_out[c] = jnp.where(lane == RATE, rate[...], x)
    fill_messages(spec_out, aux_out, outs, 2 * FAR)


def advect(half, rows, specs, aux, from_w, from_e, aux_w, aux_e, speeds, out, out_first, scratch):
    s0, s1, wet, gx, gy, field = scratch
    tiles = rows // 8
    start, width = HALVES[half]
    for c in range(EXT):
        if HALO <= c < HALO + OWN:
            x = aux[c - HALO]
            s0[c] = wide(x, 0)
            s1[c] = wide(x, LAYERS)
            wet[c] = wide(x, WET)
        else:
            ref, k = (aux_w, c) if c < HALO else (aux_e, c - HALO - OWN)
            x = ref[ref.shape[0] - 8 :, :LANES]
            for t in range(tiles):
                first = 3 * (k * tiles + t)
                at = pl.ds(8 * t, 8)
                s0[c, at] = wide(x, first)
                s1[c, at] = wide(x, first + 1)
                wet[c, at] = wide(x, first + 2)

    def store(b, c, base, x):
        n = x.shape[0]
        field[b, c, 8 + base : 8 + base + n] = x
        if base == 0:
            field[b, c, 8 + rows :] = x[:8]
        if base + n == rows:
            field[b, c, :8] = x[n - 8 :]

    def body(j, _):
        here_at = pl.ds(pl.multiple_of(j * LANES, LANES), LANES)
        spec_at = pl.ds(pl.multiple_of(start + j * LANES, LANES), LANES)
        along_x = speeds[0:1, spec_at]
        along_y = speeds[1:2, spec_at]
        for c in range(EXT):
            base = 0
            for p, piece in enumerate(specs):
                n = piece.shape[1]
                if c < HALO:
                    x = from_w[p][c * n : (c + 1) * n, here_at]
                elif c < HALO + OWN:
                    x = piece[c - HALO, :, spec_at]
                else:
                    k = c - HALO - OWN
                    x = from_e[p][k * n : (k + 1) * n, here_at]
                store(1, c, base, x)
                base += n
        for c in range(1, EXT - 1):
            w = wet[c]
            gx[c] = w * (along_x + s0[c])
            gy[c] = w * (along_y + s1[c])
        for sub in range(SUBSTEPS):
            b = (sub + 1) % 2
            mid = pl.ds(8, rows)
            before = field[b, sub, mid]
            here = field[b, sub + 1, mid]
            for c in range(sub + 1, EXT - sub - 1):
                after = field[b, c + 1, mid]
                x, y = gx[c], gy[c]
                from_x = jnp.where(x > 0.0, before, after)
                from_y = jnp.where(y > 0.0, field[b, c, 7 : 7 + rows], field[b, c, 9 : 9 + rows])
                new = here - jnp.abs(x) * (here - from_x) - jnp.abs(y) * (here - from_y)
                if sub < SUBSTEPS - 1:
                    store(sub % 2, c, 0, new)
                else:
                    at = pl.ds(pl.multiple_of(out_first + j * LANES, LANES), LANES)
                    out[c - HALO, :, at] = shrink(new, rows)
                before, here = here, after
        return 0

    lax.fori_loop(0, width // LANES, body, 0)


def first_kernel(rows, pieces, *refs):
    refs = list(refs)
    take = lambda n: [refs.pop(0) for _ in range(n)]
    specs, (aux,), from_w, from_e, (speeds, out) = take(pieces), take(1), take(pieces), take(pieces), take(2)
    advect(0, rows, specs, aux, from_w, from_e, from_w[-1], from_e[-1], speeds, out, 0, refs)


def second_kernel(rows, pieces, last, *refs):
    refs = list(refs)
    take = lambda n: [refs.pop(0) for _ in range(n)]
    specs, (aux,), from_w, from_e = take(pieces), take(1), take(pieces), take(pieces)
    (aux_w, aux_e, speeds, done, ocean, mixing, w_gate, w_up, w_down, profile) = take(10)
    spec_out, ocean_out = take(2)
    if not last:
        (aux_out,), messages = take(1), take(4)
    act, hidden = take(2)
    split = HALVES[1][0]
    fewer = rows - 2 * HALO
    advect(1, rows, specs, aux, from_w, from_e, aux_w, aux_e, speeds, spec_out, split, refs)
    wet = refs[2]

    for c in range(OWN):
        at = pl.ds(c * fewer, fewer)
        act[at, :split] = done[c].astype(jnp.bfloat16)
        act[at, split:] = spec_out[c, :, split:].astype(jnp.bfloat16)
    for n in range(0, K, CHUNK):
        a = act[...]
        gate = jnp.dot(a, w_gate[:, n : n + CHUNK], preferred_element_type=jnp.float32)
        up = jnp.dot(a, w_up[:, n : n + CHUNK], preferred_element_type=jnp.float32)
        hidden[:, n : n + CHUNK] = (jax.nn.silu(gate) * up).astype(jnp.bfloat16)
    for n, size in ((0, 384), (384, 256), (640, 256), (896, 256)):
        source = jnp.dot(hidden[...], w_down[:, n : n + size], preferred_element_type=jnp.float32)
        for c in range(OWN):
            mask = shrink(wet[c + HALO], rows)[:, :1]
            at = pl.ds(c * fewer, fewer)
            old = done[c, :, n : n + size] if n < split else spec_out[c, :, n : n + size]
            fresh = mask * (old + source[c * fewer : (c + 1) * fewer])
            spec_out[c, :, n : n + size] = fresh
            act[at, n : n + size] = fresh.astype(jnp.bfloat16)
    stokes = jnp.dot(act[...], profile[...], preferred_element_type=jnp.float32)

    lane = lax.broadcasted_iota(jnp.int32, (fewer, LANES), 1)
    first = lane < LAYERS
    kappa = mixing[...]
    for c in range(OWN):
        v = shrink(ocean[c], rows)
        known = shrink(aux[c], rows)
        lower = jnp.where((lane == 0) | (lane == LAYERS), v, pltpu.roll(v, 1, 1))
        upper = jnp.where((lane == LAYERS - 1) | (lane == 2 * LAYERS - 1), v, pltpu.roll(v, LANES - 1, 1))
        lap = lower - 2.0 * v + upper
        moved = v + stokes[c * fewer : (c + 1) * fewer]
        other = jnp.where(first, pltpu.roll(moved, LANES - LAYERS, 1), -pltpu.roll(moved, LAYERS, 1))
        new = wide(known, WET) * (v + kappa * lap + wide(known, RATE) * other)
        ocean_out[c] = new
        if not last:
            aux_out[c] = jnp.where(lane < 2 * LAYERS, 0.2 * jnp.tanh(new), known)
    if not last:
        fill_messages(spec_out, aux_out, messages, fewer)


def kernel_call(body, outs, scratch, *args, flops=0):
    block = pl.BlockSpec(memory_space=pltpu.VMEM)
    return pl.pallas_call(
        body,
        out_shape=[jax.ShapeDtypeStruct(shape, jnp.float32) for shape in outs],
        in_specs=[block] * len(args),
        out_specs=[block] * len(outs),
        scratch_shapes=scratch,
        compiler_params=pltpu.CompilerParams(vmem_limit_bytes=14 << 20),
        cost_estimate=pl.CostEstimate(flops=flops, bytes_accessed=1 << 20, transcendentals=0),
    )(*args)


def shards(
    spectrum, land, currents, group_courant, w_gate, w_up, w_down, stokes_profile, ocean_vel, mixing
):
    rows, columns, _ = spectrum.shape
    bands, sectors = lax.axis_size("sec"), lax.axis_size("comp")
    band = lax.axis_index("sec")
    up = [(i, (i + 1) % bands) for i in range(bands)]
    down = [(b, a) for a, b in up]
    east = [(i, (i + 1) % sectors) for i in range(sectors)]
    west = [(b, a) for a, b in east]

    def send_columns(messages):
        from_w = [lax.ppermute(m, "comp", east) for m in messages[:2]]
        from_e = [lax.ppermute(m, "comp", west) for m in messages[2:]]
        return from_w, from_e

    wet = land.astype(jnp.float32)
    spec = (spectrum * wet[:, :, None]).transpose(1, 0, 2)
    low, high = kernel_call(pack_rows, [(columns * FAR, K)] * 2, [], spec)
    low = lax.ppermute(low, "sec", up)
    high = lax.ppermute(high, "sec", down)
    own = send_columns(kernel_call(pack_own, message_shapes(rows, 0), [], spec))

    ocean = ocean_vel.transpose(3, 2, 0, 1).reshape(columns, rows, 2 * LAYERS)
    wet3 = wet.T[:, :, None]
    flow = jnp.moveaxis(currents, 0, 2).transpose(1, 0, 2)
    zeros = jnp.zeros((columns, rows, LANES - 2 * LAYERS - 4), jnp.float32)
    more = jnp.concatenate([ocean, wet3, wet3, flow, zeros], axis=2)
    more_low = lax.ppermute(more[:, rows - FAR :].reshape(columns * FAR, LANES), "sec", up)
    more_high = lax.ppermute(more[:, :FAR].reshape(columns * FAR, LANES), "sec", down)

    tall = rows + 2 * FAR
    places = jnp.concatenate([jnp.arange(rows + FAR), jnp.arange(-FAR, 0)])
    places = (band * rows + places).astype(jnp.float32)
    rate = 0.5 * jnp.sin((places + 0.5) * (math.pi / (rows * bands)) - math.pi / 2)
    rate = jnp.broadcast_to(rate[:, None], (tall, LANES))
    keep = jnp.stack([band > 0, band < bands - 1]).astype(jnp.float32)
    keep = jnp.broadcast_to(jnp.pad(keep, (0, 6))[:, None], (8, LANES))

    theta = 2.0 * math.pi * (jnp.arange(DIRS).astype(jnp.float32) + 0.5) / DIRS
    speed = jnp.repeat(group_courant, DIRS)
    speeds = jnp.stack([speed * jnp.tile(jnp.cos(theta), FREQS), speed * jnp.tile(jnp.sin(theta), FREQS)])
    speeds = jnp.pad(speeds, ((0, 6), (0, 0)))
    kappa = jnp.pad(jnp.concatenate([mixing, mixing]), (0, LANES - 2 * LAYERS))[None, :]
    profile = jnp.pad(stokes_profile, ((0, 0), (0, LANES - 2 * LAYERS)))

    small = (columns, tall, LANES)
    far, aux, ocean, *messages = kernel_call(
        pack_far,
        [(columns, 2 * FAR, K), small, small, *message_shapes(2 * FAR)],
        [],
        low, high, more_low, more_high, keep, rate, more,
    )
    specs = [spec, far]
    arrived = [own, send_columns(messages)]
    for step in range(STEPS):
        last = step == STEPS - 1
        fewer = tall - 2 * HALO
        pieces = len(specs)
        plane = (EXT, tall, LANES)
        scratch = [pltpu.VMEM(plane, jnp.float32)] * 5 + [
            pltpu.VMEM((2, EXT, tall + 16, LANES), jnp.float32),
        ]
        matmul = [pltpu.VMEM((columns * fewer, K), jnp.bfloat16)] * 2
        from_w = [[a[0][half] for a in arrived] for half in range(2)]
        from_e = [[a[1][half] for a in arrived] for half in range(2)]
        (done,) = kernel_call(
            functools.partial(first_kernel, tall, pieces),
            [(columns, fewer, HALVES[0][1])],
            scratch,
            *specs, aux, *from_w[0], *from_e[0], speeds,
            flops=1 << 31,
        )
        small = (columns, fewer, LANES)
        outs = [(columns, fewer, K), small]
        if not last:
            outs += [small, *message_shapes(fewer)]
        result = kernel_call(
            functools.partial(second_kernel, tall, pieces, last),
            outs,
            matmul + scratch,
            *specs, aux, *from_w[1], *from_e[1], from_w[0][-1], from_e[0][-1],
            speeds, done, ocean, kappa, w_gate, w_up, w_down, profile,
            flops=1 << 32,
        )
        spec, ocean = result[:2]
        if not last:
            aux, messages = result[2], result[3:]
            specs, arrived = [spec], [send_columns(messages)]
        tall = fewer
    spec = spec.transpose(1, 0, 2)
    ocean = ocean[:, :, : 2 * LAYERS].reshape(columns, rows, 2, LAYERS).transpose(2, 3, 1, 0)
    return spec, ocean


def solution(mesh):
    return jax.shard_map(
        shards,
        mesh=mesh,
        in_specs=(
            P("sec", "comp", None),
            P("sec", "comp"),
            P(None, "sec", "comp"),
            P(),
            P(),
            P(),
            P(),
            P(),
            P(None, None, "sec", "comp"),
            P(),
        ),
        out_specs=(P("sec", "comp", None), P(None, None, "sec", "comp")),
        check_vma=False,
    )
```

```python
import functools
import math

import jax
import jax.numpy as jnp
from jax import lax
from jax.experimental import pallas as pl
from jax.experimental.pallas import tpu as pltpu
from jax.sharding import PartitionSpec as P


DIRS = 36
FREQS = 32
K = DIRS * FREQS
LAYERS = 40
SUBSTEPS = 4
STEPS = 3
HALO = SUBSTEPS
FAR = STEPS * HALO
OWN = 6
EXT = OWN + 2 * HALO
LANES = 128
FULL = K + LANES
WET = 80
FLOW = 82
CHUNK = 384
HALVES = ((0, 640), (640, 512))


def shrink(x, rows):
    if rows == 48:
        return jnp.concatenate([x[:32], x[40:]], axis=0)
    if rows == 40:
        low = lax.broadcasted_iota(jnp.int32, (8, x.shape[1]), 0) < 4
        return jnp.concatenate([x[:24], jnp.where(low, x[24:32], x[32:])], axis=0)
    return x[:24]


def wide(x, lane):
    return jnp.broadcast_to(x[:, lane : lane + 1], (x.shape[0], LANES))


def pack_aux(cols, sources):
    tiles = cols[0].shape[0] // 8
    lane = lax.broadcasted_iota(jnp.int32, (8, LANES), 1)
    out = jnp.zeros((8, LANES), jnp.float32)
    for c, col in enumerate(cols):
        for t in range(tiles):
            part = col[8 * t : 8 * t + 8]
            first = 3 * (c * tiles + t)
            for k, source in enumerate(sources):
                out = jnp.where(lane == first + k, wide(part, source), out)
    return out


def fill_messages(state, outs, rows):
    for side, first in ((0, 2), (1, 0)):
        for half, (start, width) in enumerate(HALVES):
            for c in range(HALO):
                outs[2 * side + half][c * rows : (c + 1) * rows, :] = state[first + c, :, start : start + width]


def message_shapes(rows):
    sizes = [(HALO * rows + (0 if half else 8), width) for half, (_, width) in enumerate(HALVES)]
    return sizes * 2


def enter(spec, land, flow, ocean, state, low, high, square):
    rows = spec.shape[1]
    lane = lax.broadcasted_iota(jnp.int32, (rows, LANES), 1)
    square[...] = jnp.zeros_like(square)
    square[:OWN, :rows] = land[...].astype(jnp.float32)
    for c in range(OWN):
        square[8 + c : 9 + c, :rows] = flow[c, 0:1]
        square[16 + c : 17 + c, :rows] = flow[c, 1:2]
    points = square[...].T[:rows]
    for c in range(OWN):
        state[c, :, :K] = spec[c] * points[:, c : c + 1]
        x = jnp.where(
            lane < 2 * LAYERS + 2,
            wide(points, c),
            jnp.where(lane == FLOW, wide(points, 8 + c), wide(points, 16 + c)),
        )
        state[c, :, K:] = x
        state[c, :, K : K + LAYERS] = ocean[0, c]
        state[c, :, K + LAYERS : K + 2 * LAYERS] = ocean[1, c]
        at = pl.ds(c * FAR, FAR)
        low[at] = state[c, rows - FAR :]
        high[at] = state[c, :FAR]


def pack_own(state, east, west):
    rows = state.shape[1]
    for c in range(HALO):
        east[c * rows : (c + 1) * rows] = state[2 + c, :, :K]
        west[c * rows : (c + 1) * rows] = state[c, :, :K]


def pack_far(own, low, high, far, *outs):
    band = lax.axis_index("sec")
    keep_low = jnp.where(band > 0, 1.0, 0.0)
    keep_high = jnp.where(band < lax.axis_size("sec") - 1, 1.0, 0.0)
    for c in range(OWN):
        at = pl.ds(c * FAR, FAR)
        far[c, :FAR] = high[at] * keep_high
        far[c, FAR:] = low[at] * keep_low
    fill_messages(far, outs, 2 * FAR)
    both = [jnp.concatenate([own[c, :, K:], far[c, :, K:]], axis=0) for c in range(OWN)]
    for side, first in ((0, 2), (1, 0)):
        tile = pack_aux(both[first : first + HALO], (FLOW, FLOW + 1, WET))
        outs[2 * side][HALO * 2 * FAR :, :LANES] = tile


def advect(half, rows, first, states, from_w, from_e, aux_w, aux_e, speeds, out, out_first, scratch):
    s0, s1, wet, gx, gy, field = scratch
    tiles = rows // 8
    start, width = HALVES[half]
    for c in range(EXT):
        if HALO <= c < HALO + OWN:
            x = jnp.concatenate([piece[c - HALO, :, K:] for piece in states], axis=0)
            wet[c] = wide(x, WET)
            y = x if first else 0.2 * jnp.tanh(x)
            s0[c] = wide(y, FLOW if first else 0)
            s1[c] = wide(y, FLOW + 1 if first else LAYERS)
        else:
            ref, k = (aux_w, c) if c < HALO else (aux_e, c - HALO - OWN)
            x = ref[ref.shape[0] - 8 :, :LANES]
            for t in range(tiles):
                lane = 3 * (k * tiles + t)
                at = pl.ds(8 * t, 8)
                s0[c, at] = wide(x, lane)
                s1[c, at] = wide(x, lane + 1)
                wet[c, at] = wide(x, lane + 2)

    def store(b, c, base, x):
        n = x.shape[0]
        field[b, c, 8 + base : 8 + base + n] = x
        if base == 0:
            field[b, c, 8 + rows :] = x[:8]
        if base + n == rows:
            field[b, c, :8] = x[n - 8 :]

    def body(j, _):
        here_at = pl.ds(pl.multiple_of(j * LANES, LANES), LANES)
        spec_at = pl.ds(pl.multiple_of(start + j * LANES, LANES), LANES)
        along_x = speeds[0:1, spec_at]
        along_y = speeds[1:2, spec_at]
        for c in range(EXT):
            base = 0
            for p, piece in enumerate(states):
                n = piece.shape[1]
                if HALO <= c < HALO + OWN:
                    x = piece[c - HALO, :, spec_at]
                else:
                    ref, k = (from_w[p], c) if c < HALO else (from_e[p], c - HALO - OWN)
                    x = ref[k * n : (k + 1) * n, spec_at if ref.shape[1] == K else here_at]
                store(1, c, base, x)
                base += n
        for c in range(1, EXT - 1):
            w = wet[c]
            gx[c] = w * (along_x + s0[c])
            gy[c] = w * (along_y + s1[c])
        for sub in range(SUBSTEPS):
            b = (sub + 1) % 2
            mid = pl.ds(8, rows)
            before = field[b, sub, mid]
            here = field[b, sub + 1, mid]
            for c in range(sub + 1, EXT - sub - 1):
                after = field[b, c + 1, mid]
                x, y = gx[c], gy[c]
                from_x = jnp.where(x > 0.0, before, after)
                from_y = jnp.where(y > 0.0, field[b, c, 7 : 7 + rows], field[b, c, 9 : 9 + rows])
                new = here - jnp.abs(x) * (here - from_x) - jnp.abs(y) * (here - from_y)
                if sub < SUBSTEPS - 1:
                    store(sub % 2, c, 0, new)
                else:
                    at = pl.ds(pl.multiple_of(out_first + j * LANES, LANES), LANES)
                    out[c - HALO, :, at] = shrink(new, rows)
                before, here = here, after
        return 0

    lax.fori_loop(0, width // LANES, body, 0)


def first_kernel(rows, pieces, *refs):
    refs = list(refs)
    take = lambda n: [refs.pop(0) for _ in range(n)]
    states, from_w, from_e, (speeds, out) = take(pieces), take(pieces), take(pieces), take(2)
    advect(0, rows, pieces > 1, states, from_w, from_e, from_w[-1], from_e[-1], speeds, out, 0, refs)


def second_kernel(rows, pieces, last, *refs):
    refs = list(refs)
    take = lambda n: [refs.pop(0) for _ in range(n)]
    states, from_w, from_e = take(pieces), take(pieces), take(pieces)
    (aux_w, aux_e, speeds, done, rate, mixing, w_gate, w_up, w_down, profile, state_out) = take(11)
    if last:
        (ocean_out,) = take(1)
    else:
        messages = take(4)
    act, hidden = take(2)
    split = HALVES[1][0]
    fewer = rows - 2 * HALO
    advect(1, rows, pieces > 1, states, from_w, from_e, aux_w, aux_e, speeds, state_out, split, refs)
    wet = refs[2]

    for c in range(OWN):
        at = pl.ds(c * fewer, fewer)
        act[at, :split] = done[c].astype(jnp.bfloat16)
        act[at, split:] = state_out[c, :, split:K].astype(jnp.bfloat16)
    for n in range(0, K, CHUNK):
        a = act[...]
        gate = jnp.dot(a, w_gate[:, n : n + CHUNK], preferred_element_type=jnp.float32)
        up = jnp.dot(a, w_up[:, n : n + CHUNK], preferred_element_type=jnp.float32)
        hidden[:, n : n + CHUNK] = (jax.nn.silu(gate) * up).astype(jnp.bfloat16)
    for n, size in ((0, 384), (384, 256), (640, 256), (896, 256)):
        source = jnp.dot(hidden[...], w_down[:, n : n + size], preferred_element_type=jnp.float32)
        for c in range(OWN):
            mask = shrink(wet[c + HALO], rows)[:, :1]
            at = pl.ds(c * fewer, fewer)
            old = done[c, :, n : n + size] if n < split else state_out[c, :, n : n + size]
            fresh = mask * (old + source[c * fewer : (c + 1) * fewer])
            state_out[c, :, n : n + size] = fresh
            act[at, n : n + size] = fresh.astype(jnp.bfloat16)
    stokes = jnp.dot(act[...], profile[...], preferred_element_type=jnp.float32)

    lane = lax.broadcasted_iota(jnp.int32, (fewer, LANES), 1)
    east = lane < LAYERS
    kappa = mixing[...]
    speed = rate[...]
    for r in range(rate.shape[0], rows - 1, -2 * HALO):
        speed = shrink(speed, r)
    surf = []
    for c in range(OWN):
        v = shrink(jnp.concatenate([piece[c, :, K:] for piece in states], axis=0), rows)
        lower = jnp.where((lane == 0) | (lane == LAYERS), v, pltpu.roll(v, 1, 1))
        upper = jnp.where((lane == LAYERS - 1) | (lane == 2 * LAYERS - 1), v, pltpu.roll(v, LANES - 1, 1))
        lap = lower - 2.0 * v + upper
        moved = v + stokes[c * fewer : (c + 1) * fewer]
        other = jnp.where(east, pltpu.roll(moved, LANES - LAYERS, 1), -pltpu.roll(moved, LAYERS, 1))
        new = wide(v, WET) * (v + kappa * lap + speed * other)
        if last:
            ocean_out[0, c] = new[:, :LAYERS]
            ocean_out[1, c] = new[:, LAYERS : 2 * LAYERS]
        else:
            new = jnp.where(lane < 2 * LAYERS, new, v)
            state_out[c, :, K:] = new
            surf.append(jnp.where(lane < 2 * LAYERS, 0.2 * jnp.tanh(new), v))
    if not last:
        fill_messages(state_out, messages, fewer)
        for side, first in ((0, 2), (1, 0)):
            tile = pack_aux(surf[first : first + HALO], (0, LAYERS, WET))
            messages[2 * side][HALO * fewer :, :LANES] = tile


def kernel_call(body, outs, scratch, *args, flops=0):
    block = pl.BlockSpec(memory_space=pltpu.VMEM)
    return pl.pallas_call(
        body,
        out_shape=[jax.ShapeDtypeStruct(shape, jnp.float32) for shape in outs],
        in_specs=[block] * len(args),
        out_specs=[block] * len(outs),
        scratch_shapes=scratch,
        compiler_params=pltpu.CompilerParams(vmem_limit_bytes=14 << 20),
        cost_estimate=pl.CostEstimate(flops=flops, bytes_accessed=1 << 20, transcendentals=0),
    )(*args)


def shards(
    spectrum, land, currents, group_courant, w_gate, w_up, w_down, stokes_profile, ocean_vel, mixing
):
    rows, columns, _ = spectrum.shape
    bands, sectors = lax.axis_size("sec"), lax.axis_size("comp")
    band = lax.axis_index("sec")
    up = [(i, (i + 1) % bands) for i in range(bands)]
    down = [(b, a) for a, b in up]
    east = [(i, (i + 1) % sectors) for i in range(sectors)]
    west = [(b, a) for a, b in east]

    def send_columns(messages):
        half = len(messages) // 2
        from_w = [lax.ppermute(m, "comp", east) for m in messages[:half]]
        from_e = [lax.ppermute(m, "comp", west) for m in messages[half:]]
        return [from_w[0], from_w[-1]], [from_e[0], from_e[-1]]

    edge = (columns * FAR, FULL)
    state, low, high = kernel_call(
        enter,
        [(columns, rows, FULL), edge, edge],
        [pltpu.VMEM((LANES, LANES), jnp.float32)],
        spectrum.transpose(1, 0, 2), land.T, currents.transpose(2, 0, 1), ocean_vel.transpose(0, 3, 2, 1),
    )
    low = lax.ppermute(low, "sec", up)
    high = lax.ppermute(high, "sec", down)
    own = send_columns(kernel_call(pack_own, [(HALO * rows, K)] * 2, [], state))

    tall = rows + 2 * FAR
    places = jnp.concatenate([jnp.arange(rows + FAR), jnp.arange(-FAR, 0)])
    places = (band * rows + places).astype(jnp.float32)
    rate = 0.5 * jnp.sin((places + 0.5) * (math.pi / (rows * bands)) - math.pi / 2)
    rate = jnp.broadcast_to(rate[:, None], (tall, LANES))

    theta = 2.0 * math.pi * (jnp.arange(DIRS).astype(jnp.float32) + 0.5) / DIRS
    speed = jnp.repeat(group_courant, DIRS)
    speeds = jnp.stack([speed * jnp.tile(jnp.cos(theta), FREQS), speed * jnp.tile(jnp.sin(theta), FREQS)])
    speeds = jnp.pad(speeds, ((0, 6), (0, 0)))
    kappa = jnp.pad(jnp.concatenate([mixing, mixing]), (0, LANES - 2 * LAYERS))[None, :]
    profile = jnp.pad(stokes_profile, ((0, 0), (0, LANES - 2 * LAYERS)))

    far, *messages = kernel_call(
        pack_far, [(columns, 2 * FAR, FULL), *message_shapes(2 * FAR)], [], state, low, high
    )
    states = [state, far]
    arrived = [own, send_columns(messages)]
    for step in range(STEPS):
        last = step == STEPS - 1
        fewer = tall - 2 * HALO
        pieces = len(states)
        plane = (EXT, tall, LANES)
        scratch = [pltpu.VMEM(plane, jnp.float32)] * 5 + [
            pltpu.VMEM((2, EXT, tall + 16, LANES), jnp.float32),
        ]
        matmul = [pltpu.VMEM((columns * fewer, K), jnp.bfloat16)] * 2
        from_w = [[a[0][half] for a in arrived] for half in range(2)]
        from_e = [[a[1][half] for a in arrived] for half in range(2)]
        (done,) = kernel_call(
            functools.partial(first_kernel, tall, pieces),
            [(columns, fewer, HALVES[0][1])],
            scratch,
            *states, *from_w[0], *from_e[0], speeds,
            flops=1 << 31,
        )
        if last:
            outs = [(columns, fewer, K), (2, columns, fewer, LAYERS)]
        else:
            outs = [(columns, fewer, FULL), *message_shapes(fewer)]
        result = kernel_call(
            functools.partial(second_kernel, tall, pieces, last),
            outs,
            matmul + scratch,
            *states, *from_w[1], *from_e[1], from_w[0][-1], from_e[0][-1],
            speeds, done, rate, kappa, w_gate, w_up, w_down, profile,
            flops=1 << 32,
        )
        if not last:
            states, arrived = [result[0]], [send_columns(result[1:])]
        tall = fewer
    spec, ocean = result
    return spec.transpose(1, 0, 2), ocean.transpose(0, 3, 2, 1)


def solution(mesh):
    return jax.shard_map(
        shards,
        mesh=mesh,
        in_specs=(
            P("sec", "comp", None),
            P("sec", "comp"),
            P(None, "sec", "comp"),
            P(),
            P(),
            P(),
            P(),
            P(),
            P(None, None, "sec", "comp"),
            P(),
        ),
        out_specs=(P("sec", "comp", None), P(None, None, "sec", "comp")),
        check_vma=False,
    )
```

```python
import functools
import math

import jax
import jax.numpy as jnp
from jax import lax
from jax.experimental import pallas as pl
from jax.experimental.pallas import tpu as pltpu
from jax.sharding import PartitionSpec as P


DIRS = 36
FREQS = 32
K = DIRS * FREQS
LAYERS = 40
SUBSTEPS = 4
STEPS = 3
NLAT = 96
BANDS = 4
HALO = SUBSTEPS
FAR = STEPS * HALO
OWN = 6
EXT = OWN + 2 * HALO
LANES = 128
FULL = K + LANES
WET = 80
FLOW = 82
CHUNK = 384
HALVES = ((0, 640), (640, 512))


def shrink(x, rows):
    if rows == 48:
        return jnp.concatenate([x[:32], x[40:]], axis=0)
    if rows == 40:
        low = lax.broadcasted_iota(jnp.int32, (8, x.shape[1]), 0) < 4
        return jnp.concatenate([x[:24], jnp.where(low, x[24:32], x[32:])], axis=0)
    return x[:24]


def wide(x, lane):
    return jnp.broadcast_to(x[:, lane : lane + 1], (x.shape[0], LANES))


def pack_aux(cols, sources):
    tiles = cols[0].shape[0] // 8
    lane = lax.broadcasted_iota(jnp.int32, (8, LANES), 1)
    out = jnp.zeros((8, LANES), jnp.float32)
    for c, col in enumerate(cols):
        for t in range(tiles):
            part = col[8 * t : 8 * t + 8]
            first = 3 * (c * tiles + t)
            for k, source in enumerate(sources):
                out = jnp.where(lane == first + k, wide(part, source), out)
    return out


def fill_messages(state, outs, rows):
    for side, first in ((0, 2), (1, 0)):
        for half, (start, width) in enumerate(HALVES):
            for c in range(HALO):
                outs[2 * side + half][c * rows : (c + 1) * rows, :] = state[first + c, :, start : start + width]


def message_shapes(rows):
    sizes = [(HALO * rows + (0 if half else 8), width) for half, (_, width) in enumerate(HALVES)]
    return sizes * 2


def enter(*refs):
    sources, (state, low, high, group_out, square), copies, sems = refs[:5], refs[5:10], refs[10:15], refs[15]
    moves = [pltpu.make_async_copy(a, b, sems.at[i]) for i, (a, b) in enumerate(zip(sources, copies))]
    for move in moves:
        move.start()
    spec, land, flow, ocean, group = copies
    rows = spec.shape[1]
    lane = lax.broadcasted_iota(jnp.int32, (rows, LANES), 1)
    square[...] = jnp.zeros_like(square)
    for move in moves:
        move.wait()
    square[:OWN, :rows] = land[...].astype(jnp.float32)
    for c in range(OWN):
        square[8 + c : 9 + c, :rows] = flow[c, 0:1]
        square[16 + c : 17 + c, :rows] = flow[c, 1:2]
    points = square[...].T[:rows]
    for c in range(OWN):
        state[c, :, :K] = spec[c] * points[:, c : c + 1]
        x = jnp.where(
            lane < 2 * LAYERS + 2,
            wide(points, c),
            jnp.where(lane == FLOW, wide(points, 8 + c), wide(points, 16 + c)),
        )
        state[c, :, K:] = x
        state[c, :, K : K + LAYERS] = ocean[0, c]
        state[c, :, K + LAYERS : K + 2 * LAYERS] = ocean[1, c]
        at = pl.ds(c * FAR, FAR)
        low[at] = state[c, rows - FAR :]
        high[at] = state[c, :FAR]
    group_out[...] = group[...]


def pack_own(state, group, east, west, speeds):
    rows = state.shape[1]
    place = lax.broadcasted_iota(jnp.int32, (1, K), 1).astype(jnp.float32)
    speed = jnp.zeros((1, K), jnp.float32)
    turn = place
    for f in range(FREQS):
        later = place >= f * DIRS
        speed = jnp.where(later, group[0:1, f : f + 1], speed)
        turn = jnp.where(later, place - f * DIRS, turn)
    theta = 2.0 * math.pi * (turn + 0.5) / DIRS
    speeds[0:1] = speed * jnp.cos(theta)
    speeds[1:2] = speed * jnp.sin(theta)
    for c in range(HALO):
        east[c * rows : (c + 1) * rows] = state[2 + c, :, :K]
        west[c * rows : (c + 1) * rows] = state[c, :, :K]


def pack_far(own, low, high, far, *outs):
    band = lax.axis_index("sec")
    keep_low = jnp.where(band > 0, 1.0, 0.0)
    keep_high = jnp.where(band < lax.axis_size("sec") - 1, 1.0, 0.0)
    for c in range(OWN):
        at = pl.ds(c * FAR, FAR)
        far[c, :FAR] = high[at] * keep_high
        far[c, FAR:] = low[at] * keep_low
    fill_messages(far, outs, 2 * FAR)
    both = [jnp.concatenate([own[c, :, K:], far[c, :, K:]], axis=0) for c in range(OWN)]
    for side, first in ((0, 2), (1, 0)):
        tile = pack_aux(both[first : first + HALO], (FLOW, FLOW + 1, WET))
        outs[2 * side][HALO * 2 * FAR :, :LANES] = tile


def advect(half, rows, first, states, from_w, from_e, aux_w, aux_e, speeds, out, out_first, scratch):
    s0, s1, wet, gx, gy, field = scratch
    tiles = rows // 8
    start, width = HALVES[half]
    for c in range(EXT):
        if HALO <= c < HALO + OWN:
            x = jnp.concatenate([piece[c - HALO, :, K:] for piece in states], axis=0)
            wet[c] = wide(x, WET)
            y = x if first else 0.2 * jnp.tanh(x)
            s0[c] = wide(y, FLOW if first else 0)
            s1[c] = wide(y, FLOW + 1 if first else LAYERS)
        else:
            ref, k = (aux_w, c) if c < HALO else (aux_e, c - HALO - OWN)
            x = ref[ref.shape[0] - 8 :, :LANES]
            for t in range(tiles):
                lane = 3 * (k * tiles + t)
                at = pl.ds(8 * t, 8)
                s0[c, at] = wide(x, lane)
                s1[c, at] = wide(x, lane + 1)
                wet[c, at] = wide(x, lane + 2)

    def store(b, c, base, x):
        n = x.shape[0]
        field[b, c, 8 + base : 8 + base + n] = x
        if base == 0:
            field[b, c, 8 + rows :] = x[:8]
        if base + n == rows:
            field[b, c, :8] = x[n - 8 :]

    def body(j, _):
        here_at = pl.ds(pl.multiple_of(j * LANES, LANES), LANES)
        spec_at = pl.ds(pl.multiple_of(start + j * LANES, LANES), LANES)
        along_x = speeds[0:1, spec_at]
        along_y = speeds[1:2, spec_at]
        for c in range(EXT):
            base = 0
            for p, piece in enumerate(states):
                n = piece.shape[1]
                if HALO <= c < HALO + OWN:
                    x = piece[c - HALO, :, spec_at]
                else:
                    ref, k = (from_w[p], c) if c < HALO else (from_e[p], c - HALO - OWN)
                    x = ref[k * n : (k + 1) * n, spec_at if ref.shape[1] == K else here_at]
                store(1, c, base, x)
                base += n
        for c in range(1, EXT - 1):
            w = wet[c]
            gx[c] = w * (along_x + s0[c])
            gy[c] = w * (along_y + s1[c])
        for sub in range(SUBSTEPS):
            b = (sub + 1) % 2
            mid = pl.ds(8, rows)
            before = field[b, sub, mid]
            here = field[b, sub + 1, mid]
            for c in range(sub + 1, EXT - sub - 1):
                after = field[b, c + 1, mid]
                x, y = gx[c], gy[c]
                from_x = jnp.where(x > 0.0, before, after)
                from_y = jnp.where(y > 0.0, field[b, c, 7 : 7 + rows], field[b, c, 9 : 9 + rows])
                new = here - jnp.abs(x) * (here - from_x) - jnp.abs(y) * (here - from_y)
                if sub < SUBSTEPS - 1:
                    store(sub % 2, c, 0, new)
                else:
                    at = pl.ds(pl.multiple_of(out_first + j * LANES, LANES), LANES)
                    out[c - HALO, :, at] = shrink(new, rows)
                before, here = here, after
        return 0

    lax.fori_loop(0, width // LANES, body, 0)


def first_kernel(rows, pieces, *refs):
    refs = list(refs)
    take = lambda n: [refs.pop(0) for _ in range(n)]
    states, from_w, from_e, (speeds, out) = take(pieces), take(pieces), take(pieces), take(2)
    advect(0, rows, pieces > 1, states, from_w, from_e, from_w[-1], from_e[-1], speeds, out, 0, refs)


def second_kernel(rows, pieces, last, *refs):
    refs = list(refs)
    take = lambda n: [refs.pop(0) for _ in range(n)]
    states, from_w, from_e = take(pieces), take(pieces), take(pieces)
    (aux_w, aux_e, speeds, done, mixing, w_gate, w_up, w_down, profile, state_out) = take(10)
    if last:
        (ocean_out,) = take(1)
    else:
        messages = take(4)
    act, hidden, wide_profile, kappas = take(4)
    split = HALVES[1][0]
    fewer = rows - 2 * HALO
    advect(1, rows, pieces > 1, states, from_w, from_e, aux_w, aux_e, speeds, state_out, split, refs)
    wet = refs[2]

    for c in range(OWN):
        at = pl.ds(c * fewer, fewer)
        act[at, :split] = done[c].astype(jnp.bfloat16)
        act[at, split:] = state_out[c, :, split:K].astype(jnp.bfloat16)
    for n in range(0, K, CHUNK):
        a = act[...]
        gate = jnp.dot(a, w_gate[:, n : n + CHUNK], preferred_element_type=jnp.float32)
        up = jnp.dot(a, w_up[:, n : n + CHUNK], preferred_element_type=jnp.float32)
        hidden[:, n : n + CHUNK] = (jax.nn.silu(gate) * up).astype(jnp.bfloat16)
    for n, size in ((0, 384), (384, 256), (640, 256), (896, 256)):
        source = jnp.dot(hidden[...], w_down[:, n : n + size], preferred_element_type=jnp.float32)
        for c in range(OWN):
            mask = shrink(wet[c + HALO], rows)[:, :1]
            at = pl.ds(c * fewer, fewer)
            old = done[c, :, n : n + size] if n < split else state_out[c, :, n : n + size]
            fresh = mask * (old + source[c * fewer : (c + 1) * fewer])
            state_out[c, :, n : n + size] = fresh
            act[at, n : n + size] = fresh.astype(jnp.bfloat16)
    layers = profile.shape[0]
    wide_profile[:layers] = profile[...]
    wide_profile[layers:] = jnp.zeros((LANES - layers, K), jnp.bfloat16)
    stokes = lax.dot_general(
        act[...], wide_profile[...], (((1,), (1,)), ((), ())), preferred_element_type=jnp.float32
    )

    lane = lax.broadcasted_iota(jnp.int32, (fewer, LANES), 1)
    east = lane < LAYERS
    kappas[:, :LAYERS] = mixing[...]
    kappas[:, LAYERS : 2 * LAYERS] = mixing[...]
    kappa = kappas[...]
    place = lax.broadcasted_iota(jnp.int32, (fewer, LANES), 0)
    reach = (fewer - NLAT // BANDS) // 2
    place = jnp.where(place < fewer - reach, place, place - fewer)
    place = (lax.axis_index("sec") * (NLAT // BANDS) + place).astype(jnp.float32)
    speed = 0.5 * jnp.sin((place + 0.5) * (math.pi / NLAT) - math.pi / 2)
    surf = []
    for c in range(OWN):
        v = shrink(jnp.concatenate([piece[c, :, K:] for piece in states], axis=0), rows)
        lower = jnp.where((lane == 0) | (lane == LAYERS), v, pltpu.roll(v, 1, 1))
        upper = jnp.where((lane == LAYERS - 1) | (lane == 2 * LAYERS - 1), v, pltpu.roll(v, LANES - 1, 1))
        lap = lower - 2.0 * v + upper
        moved = v + stokes[c * fewer : (c + 1) * fewer]
        other = jnp.where(east, pltpu.roll(moved, LANES - LAYERS, 1), -pltpu.roll(moved, LAYERS, 1))
        new = wide(v, WET) * (v + kappa * lap + speed * other)
        if last:
            ocean_out[0, c] = new[:, :LAYERS]
            ocean_out[1, c] = new[:, LAYERS : 2 * LAYERS]
        else:
            new = jnp.where(lane < 2 * LAYERS, new, v)
            state_out[c, :, K:] = new
            surf.append(jnp.where(lane < 2 * LAYERS, 0.2 * jnp.tanh(new), v))
    if not last:
        fill_messages(state_out, messages, fewer)
        for side, first in ((0, 2), (1, 0)):
            tile = pack_aux(surf[first : first + HALO], (0, LAYERS, WET))
            messages[2 * side][HALO * fewer :, :LANES] = tile


def kernel_call(body, outs, scratch, *args, flops=0, space=pltpu.VMEM):
    block = pl.BlockSpec(memory_space=pltpu.VMEM)
    return pl.pallas_call(
        body,
        out_shape=[jax.ShapeDtypeStruct(shape, jnp.float32) for shape in outs],
        in_specs=[pl.BlockSpec(memory_space=space)] * len(args),
        out_specs=[block] * len(outs),
        scratch_shapes=scratch,
        compiler_params=pltpu.CompilerParams(vmem_limit_bytes=14 << 20),
        cost_estimate=pl.CostEstimate(flops=flops, bytes_accessed=1 << 20, transcendentals=0),
    )(*args)


def shards(
    spectrum, land, currents, group_courant, w_gate, w_up, w_down, stokes_profile, ocean_vel, mixing
):
    rows, columns, _ = spectrum.shape
    bands, sectors = lax.axis_size("sec"), lax.axis_size("comp")
    up = [(i, (i + 1) % bands) for i in range(bands)]
    down = [(b, a) for a, b in up]
    east = [(i, (i + 1) % sectors) for i in range(sectors)]
    west = [(b, a) for a, b in east]

    def send_columns(messages):
        half = len(messages) // 2
        from_w = [lax.ppermute(m, "comp", east) for m in messages[:half]]
        from_e = [lax.ppermute(m, "comp", west) for m in messages[half:]]
        return [from_w[0], from_w[-1]], [from_e[0], from_e[-1]]

    edge = (columns * FAR, FULL)
    inputs = (
        spectrum.transpose(1, 0, 2),
        land.T,
        currents.transpose(2, 0, 1),
        ocean_vel.transpose(0, 3, 2, 1),
        group_courant[None],
    )
    state, low, high, group = kernel_call(
        enter,
        [(columns, rows, FULL), edge, edge, (1, FREQS)],
        [pltpu.VMEM((LANES, LANES), jnp.float32)]
        + [pltpu.VMEM(x.shape, x.dtype) for x in inputs]
        + [pltpu.SemaphoreType.DMA((len(inputs),))],
        *inputs,
        space=pltpu.HBM,
    )
    low = lax.ppermute(low, "sec", up)
    high = lax.ppermute(high, "sec", down)
    side = (HALO * rows, K)
    *messages, speeds = kernel_call(pack_own, [side, side, (8, K)], [], state, group)
    own = send_columns(messages)
    tall = rows + 2 * FAR
    far, *messages = kernel_call(
        pack_far, [(columns, 2 * FAR, FULL), *message_shapes(2 * FAR)], [], state, low, high
    )
    states = [state, far]
    arrived = [own, send_columns(messages)]
    for step in range(STEPS):
        last = step == STEPS - 1
        fewer = tall - 2 * HALO
        pieces = len(states)
        plane = (EXT, tall, LANES)
        scratch = [pltpu.VMEM(plane, jnp.float32)] * 5 + [
            pltpu.VMEM((2, EXT, tall + 16, LANES), jnp.float32),
        ]
        matmul = [pltpu.VMEM((columns * fewer, K), jnp.bfloat16)] * 2 + [
            pltpu.VMEM((LANES, K), jnp.bfloat16),
            pltpu.VMEM((1, LANES), jnp.float32),
        ]
        from_w = [[a[0][half] for a in arrived] for half in range(2)]
        from_e = [[a[1][half] for a in arrived] for half in range(2)]
        (done,) = kernel_call(
            functools.partial(first_kernel, tall, pieces),
            [(columns, fewer, HALVES[0][1])],
            scratch,
            *states, *from_w[0], *from_e[0], speeds,
            flops=1 << 31,
        )
        if last:
            outs = [(columns, fewer, K), (2, columns, fewer, LAYERS)]
        else:
            outs = [(columns, fewer, FULL), *message_shapes(fewer)]
        result = kernel_call(
            functools.partial(second_kernel, tall, pieces, last),
            outs,
            matmul + scratch,
            *states, *from_w[1], *from_e[1], from_w[0][-1], from_e[0][-1],
            speeds, done, mixing[None], w_gate, w_up, w_down, stokes_profile.T,
            flops=1 << 32,
        )
        if not last:
            states, arrived = [result[0]], [send_columns(result[1:])]
        tall = fewer
    spec, ocean = result
    return spec.transpose(1, 0, 2), ocean.transpose(0, 3, 2, 1)


def solution(mesh):
    return jax.shard_map(
        shards,
        mesh=mesh,
        in_specs=(
            P("sec", "comp", None),
            P("sec", "comp"),
            P(None, "sec", "comp"),
            P(),
            P(),
            P(),
            P(),
            P(),
            P(None, None, "sec", "comp"),
            P(),
        ),
        out_specs=(P("sec", "comp", None), P(None, None, "sec", "comp")),
        check_vma=False,
    )
```
